1024 devices in a mesh: lam: 64 (over z, y_hi, core), nu: 16 (over y_lo, x).
Axes of the slice: x: 8, y: 8 (y_hi: 4, y_lo: 2; y = y_hi * 2 + y_lo), z: 8, core: 2. Of those that a mesh axis runs over, the one named last changes fastest.
Arguments:
- integrals: bfloat16 [128, 2048, 2048], P('lam', None, 'nu'), may hold values from -6 to 6
- orbitals: bfloat16 [2048, 512], replicated, may hold values from -0.125 to 0.125
- lam_orbitals: bfloat16 [128, 4], P('lam'), may hold values from -0.5 to 0.5
Outputs:
- transformed: float32 [4, 512, 512], P(None, 'nu', 'lam')
The draws below stay inside these ranges and needn't reach their ends.
All inputs are finite; a program needn't handle non-finite values.
Results may differ from the reference program's by a relative error of at most 0.0029.
Values may be sent and summed in bfloat16 or wider, within the bound.
No kernel may reach another device: no remote copies, remote signals or barrier semaphores. Data moves between devices by JAX's collectives and lax.ppermute only.
A program may use at most 32 MiB of HBM per device.

```python
import jax
import jax.numpy as jnp
from jax import lax

NBF = 2048
NMO = 512
KORB = 4
LAM = 128


def block_scale(stream_key, dims, shards, least, largest):
    level, own = 1.0, jax.random.fold_in(stream_key, 6)
    for dim, blocks in shards:
        draws = jnp.exp(jax.random.uniform(jax.random.fold_in(own, dim), (blocks,), jnp.float32, least / len(shards), largest / len(shards)))
        level = level * jnp.repeat(draws, dims[dim] // blocks).reshape([-1 if axis == dim else 1 for axis in range(len(dims))])
    return level


def bell_draw(own_key, dims, scale, bound, shards=(), dtype=jnp.bfloat16):
    result = scale * jax.random.normal(own_key, dims, jnp.float32)
    if shards:
        result = result * block_scale(own_key, dims, shards, -0.22, 0.18)
    return jnp.clip(result, -bound, bound).astype(dtype)


def setup_inputs(seed: int = 0) -> dict:
    key_of = jax.random.split(jax.random.key(seed), 4)
    return {
        "integrals": bell_draw(key_of[0], (LAM, NBF, NBF), 1.0, 6.0, ((0, 64), (2, 16))),
        "orbitals": bell_draw(key_of[1], (NBF, NMO), NBF ** -0.5, 0.125),
        "lam_orbitals": bell_draw(key_of[2], (LAM, KORB), LAM ** -0.5, 0.5, ((0, 64),)),
    }


def reference(integrals, orbitals, lam_orbitals):
    def transform_one(running, inputs):
        ao_slab, weights = inputs
        halfway = lax.dot_general(orbitals, ao_slab, (((0,), (0,)), ((), ())), preferred_element_type=jnp.float32).astype(jnp.bfloat16)
        second = jnp.dot(halfway, orbitals, preferred_element_type=jnp.float32)
        return running + weights.astype(jnp.float32)[:, None, None] * second[None, :, :], None

    start_sum = jnp.zeros((KORB, NMO, NMO), jnp.float32)
    transformed, unused = lax.scan(transform_one, start_sum, (integrals, lam_orbitals))
    return transformed
```

```python
import jax
import jax.numpy as jnp
from jax import lax
from jax.sharding import PartitionSpec as P


def shards(integrals, orbitals, lam_orbitals):
    halfway = jnp.einsum(
        "lmn,mi->lin", integrals, orbitals, preferred_element_type=jnp.float32
    ).astype(jnp.bfloat16)
    halfway = halfway.reshape(2, 16, 32, 128).transpose(1, 0, 2, 3)
    exchanged = lax.all_to_all(halfway, "nu", split_axis=0, concat_axis=0, tiled=True)
    weights = lam_orbitals.astype(jnp.float32)
    rows = exchanged.transpose(1, 2, 0, 3).reshape(64, 2048)
    second = jnp.einsum("nj,rn->jr", orbitals, rows, preferred_element_type=jnp.float32)
    s0, s1 = second[:, :32], second[:, 32:]
    terms = jnp.concatenate([s0 * weights[0, k] + s1 * weights[1, k] for k in range(4)], axis=1)
    sent = terms.astype(jnp.bfloat16).reshape(64, 8, 128)
    received = lax.all_to_all(sent, "lam", split_axis=0, concat_axis=0, tiled=True)
    summed = jnp.sum(received.astype(jnp.float32), axis=0)
    return summed.reshape(8, 4, 32).transpose(1, 2, 0)


def solution(mesh):
    return jax.shard_map(
        shards,
        mesh=mesh,
        in_specs=(P("lam", None, "nu"), P(), P("lam", None)),
        out_specs=P(None, "nu", "lam"),
        check_vma=False,
    )
```

```python
import functools

import jax
import jax.numpy as jnp
from jax import lax
from jax.experimental import pallas as pl
from jax.experimental.pallas import tpu as pltpu
from jax.sharding import PartitionSpec as P

CHUNKS = 4
VMEM_LIMIT = 16 << 20
NU_FIRST = 12
LAM_FIRST = 36


def turned(size, start):
    return [(start + p) % size for p in range(size)]


def first_kernel(integrals_hbm, orbitals_hbm, out_ref, orbitals, integrals, sems):
    lams, mus, _ = integrals.shape
    owners = out_ref.shape[0]
    size = mus // CHUNKS
    copies = []
    for c in range(CHUNKS):
        rows = pl.ds(c * size, size)
        copies.append(
            (
                pltpu.make_async_copy(orbitals_hbm.at[rows], orbitals.at[rows], sems.at[0, c]),
                pltpu.make_async_copy(integrals_hbm.at[:, rows], integrals.at[:, rows], sems.at[1, c]),
            )
        )
    for pair in copies:
        for copy in pair:
            copy.start()
    totals = [None] * lams
    for c in range(CHUNKS):
        for copy in copies[c]:
            copy.wait()
        rows = pl.ds(c * size, size)
        block = orbitals[rows, :]
        for l in range(lams):
            term = lax.dot_general(
                block, integrals[l, rows, :], (((0,), (0,)), ((), ())), preferred_element_type=jnp.float32
            )
            totals[l] = term if c == 0 else totals[l] + term
    for l in range(lams):
        total = totals[l].astype(out_ref.dtype)
        width = total.shape[0] // owners
        for p, owner in enumerate(turned(owners, NU_FIRST)):
            out_ref[p, l * width : (l + 1) * width, :] = total[owner * width : (owner + 1) * width]


def first(integrals, orbitals, owners):
    lams, mus, ns = integrals.shape
    orbs = orbitals.shape[1]
    return pl.pallas_call(
        first_kernel,
        out_shape=(
            pltpu.VMEM((owners, lams * orbs // owners, ns), integrals.dtype),
            pltpu.VMEM(orbitals.shape, orbitals.dtype),
        ),
        in_specs=[pl.BlockSpec(memory_space=pltpu.HBM), pl.BlockSpec(memory_space=pltpu.HBM)],
        out_specs=(pl.BlockSpec(memory_space=pltpu.VMEM), pl.BlockSpec(memory_space=pltpu.VMEM)),
        scratch_shapes=[
            pltpu.VMEM(integrals.shape, integrals.dtype),
            pltpu.SemaphoreType.DMA((2, CHUNKS)),
        ],
        compiler_params=pltpu.CompilerParams(vmem_limit_bytes=VMEM_LIMIT),
    )(*(pltpu.with_memory_space_constraint(x, pltpu.HBM) for x in (integrals, orbitals)))


def second_kernel(weights_ref, rows_ref, orbitals_ref, out_ref):
    lams, korb = weights_ref.shape
    owners, height, ns = rows_ref.shape
    step = 2
    total = None
    for s in range(0, owners, step):
        left = jnp.concatenate([rows_ref[s + t] for t in range(step)], axis=1)
        owner = (s + NU_FIRST) % owners
        right = orbitals_ref[owner * ns : (owner + step) * ns, :]
        term = jnp.dot(left, right, preferred_element_type=jnp.float32)
        total = term if total is None else total + term
    width = height // lams
    weights = weights_ref[...].astype(jnp.float32)
    terms = []
    for k in range(korb):
        term = weights[0:1, k : k + 1] * total[:width]
        for l in range(1, lams):
            term = term + weights[l : l + 1, k : k + 1] * total[l * width : (l + 1) * width]
        terms.append(term)
    sent = jnp.concatenate(terms, axis=0).T
    sent = sent.reshape(out_ref.shape).astype(out_ref.dtype)
    out_ref[: out_ref.shape[0] - LAM_FIRST] = sent[LAM_FIRST:]
    out_ref[out_ref.shape[0] - LAM_FIRST :] = sent[:LAM_FIRST]


def second(weights, rows, orbitals, owners):
    _, height, _ = rows.shape
    lams, korb = weights.shape
    orbs = orbitals.shape[1]
    vmem = pl.BlockSpec(memory_space=pltpu.VMEM)
    return pl.pallas_call(
        second_kernel,
        out_shape=pltpu.VMEM((owners, orbs // owners, korb * height // lams), rows.dtype),
        in_specs=[vmem, vmem, vmem],
        out_specs=vmem,
        compiler_params=pltpu.CompilerParams(vmem_limit_bytes=VMEM_LIMIT),
    )(*(pltpu.with_memory_space_constraint(x, pltpu.VMEM) for x in (weights, rows, orbitals)))


def shards(lam_owners, nu_owners, integrals, orbitals, lam_orbitals):
    halfway, orbitals = first(integrals, orbitals, nu_owners)
    exchanged = lax.all_to_all(
        halfway, "nu", split_axis=0, concat_axis=0, tiled=True, axis_index_groups=[turned(nu_owners, NU_FIRST)]
    )
    sent = second(lam_orbitals, exchanged, orbitals, lam_owners)
    received = lax.all_to_all(
        sent, "lam", split_axis=0, concat_axis=0, tiled=True, axis_index_groups=[turned(lam_owners, LAM_FIRST)]
    )
    summed = jnp.sum(received.astype(jnp.float32), axis=0)
    korb = lam_orbitals.shape[1]
    return summed.reshape(summed.shape[0], korb, -1).transpose(1, 2, 0)


def solution(mesh):
    return jax.shard_map(
        functools.partial(shards, mesh.shape["lam"], mesh.shape["nu"]),
        mesh=mesh,
        in_specs=(P("lam", None, "nu"), P(), P("lam", None)),
        out_specs=P(None, "nu", "lam"),
        check_vma=False,
    )
```

```python
import functools

import jax
import jax.numpy as jnp
from jax import lax
from jax.experimental import pallas as pl
from jax.experimental.pallas import tpu as pltpu
from jax.sharding import PartitionSpec as P

CHUNKS = 4
VMEM_LIMIT = 16 << 20
VMEM = pl.BlockSpec(memory_space=pltpu.VMEM)
HBM = pl.BlockSpec(memory_space=pltpu.HBM)
PARAMS = pltpu.CompilerParams(vmem_limit_bytes=VMEM_LIMIT)


def nu_order(size):
    return [(12 + p) % size for p in range(size)]


def lam_order(size):
    return [(45 + p) % size for p in range(size)]


def first_kernel(integrals_hbm, orbitals_hbm, out_ref, orbitals, integrals, sems):
    lams, mus, ns = integrals.shape
    owners = out_ref.shape[0]
    size = mus // CHUNKS
    copies = []
    for c in range(CHUNKS):
        rows = pl.ds(c * size, size)
        copies.append(
            (
                pltpu.make_async_copy(orbitals_hbm.at[rows], orbitals.at[rows], sems.at[0, c]),
                pltpu.make_async_copy(integrals_hbm.at[:, rows], integrals.at[:, rows], sems.at[1, c]),
            )
        )
    for pair in copies:
        for copy in pair:
            copy.start()
    total = None
    for c in range(CHUNKS):
        for copy in copies[c]:
            copy.wait()
        rows = pl.ds(c * size, size)
        block = jnp.concatenate([integrals[l, rows, :].T for l in range(lams)], axis=0)
        term = jnp.dot(block, orbitals[rows, :], preferred_element_type=jnp.float32)
        total = term if total is None else total + term
    total = total.astype(out_ref.dtype)
    width = total.shape[1] // owners
    for l in range(lams):
        block = total[l * ns : (l + 1) * ns].T
        for p, owner in enumerate(nu_order(owners)):
            out_ref[p, l * width : (l + 1) * width, :] = block[owner * width : (owner + 1) * width]


def first(integrals, orbitals, owners):
    lams, _, ns = integrals.shape
    orbs = orbitals.shape[1]
    return pl.pallas_call(
        first_kernel,
        out_shape=(
            pltpu.VMEM((owners, lams * orbs // owners, ns), integrals.dtype),
            pltpu.VMEM(orbitals.shape, orbitals.dtype),
        ),
        in_specs=[HBM, HBM],
        out_specs=(VMEM, VMEM),
        scratch_shapes=[
            pltpu.VMEM(integrals.shape, integrals.dtype),
            pltpu.SemaphoreType.DMA((2, CHUNKS)),
        ],
        compiler_params=PARAMS,
    )(*(pltpu.with_memory_space_constraint(x, pltpu.HBM) for x in (integrals, orbitals)))


def second_kernel(weights_ref, rows_ref, orbitals_ref, out_ref):
    lams, korb = weights_ref.shape
    owners, height, ns = rows_ref.shape
    place = {owner: p for p, owner in enumerate(nu_order(owners))}
    step = 2
    total = None
    for s in range(0, owners, step):
        left = jnp.concatenate([rows_ref[place[s + t]] for t in range(step)], axis=1)
        right = orbitals_ref[s * ns : (s + step) * ns, :]
        term = jnp.dot(left, right, preferred_element_type=jnp.float32)
        total = term if total is None else total + term
    width = height // lams
    weights = weights_ref[...].astype(jnp.float32)
    terms = []
    for k in range(korb):
        term = weights[0:1, k : k + 1] * total[:width]
        for l in range(1, lams):
            term = term + weights[l : l + 1, k : k + 1] * total[l * width : (l + 1) * width]
        terms.append(term)
    sent = jnp.concatenate(terms, axis=0).T
    sent = sent.reshape(out_ref.shape).astype(out_ref.dtype)
    for p, owner in enumerate(lam_order(out_ref.shape[0])):
        out_ref[p] = sent[owner]


def second(weights, rows, orbitals, owners):
    _, height, _ = rows.shape
    lams, korb = weights.shape
    orbs = orbitals.shape[1]
    return pl.pallas_call(
        second_kernel,
        out_shape=pltpu.VMEM((owners, orbs // owners, korb * height // lams), rows.dtype),
        in_specs=[VMEM, VMEM, VMEM],
        out_specs=VMEM,
        compiler_params=PARAMS,
    )(*(pltpu.with_memory_space_constraint(x, pltpu.VMEM) for x in (weights, rows, orbitals)))


def last_kernel(terms_ref, out_ref):
    korb, _, width = out_ref.shape
    total = jnp.sum(terms_ref[...].astype(jnp.float32), axis=0)
    for k in range(korb):
        out_ref[k] = total[:, k * width : (k + 1) * width]


def last(terms, korb):
    _, js, height = terms.shape
    return pl.pallas_call(
        last_kernel,
        out_shape=jax.ShapeDtypeStruct((korb, js, height // korb), jnp.float32),
        in_specs=[VMEM],
        out_specs=VMEM,
        compiler_params=PARAMS,
    )(pltpu.with_memory_space_constraint(terms, pltpu.VMEM))


def exchange(blocks, axis, order):
    return lax.all_to_all(blocks, axis, split_axis=0, concat_axis=0, tiled=True, axis_index_groups=[order])


def shards(lam_owners, nu_owners, integrals, orbitals, lam_orbitals):
    halfway, orbitals = first(integrals, orbitals, nu_owners)
    rows = exchange(halfway, "nu", nu_order(nu_owners))
    sent = second(lam_orbitals, rows, orbitals, lam_owners)
    terms = exchange(sent, "lam", lam_order(lam_owners))
    return last(terms, lam_orbitals.shape[1]).transpose(0, 2, 1)


def solution(mesh):
    return jax.shard_map(
        functools.partial(shards, mesh.shape["lam"], mesh.shape["nu"]),
        mesh=mesh,
        in_specs=(P("lam", None, "nu"), P(), P("lam", None)),
        out_specs=P(None, "nu", "lam"),
        check_vma=False,
    )
```

```python
import functools

import jax
import jax.numpy as jnp
from jax import lax
from jax.experimental import pallas as pl
from jax.experimental.pallas import tpu as pltpu
from jax.sharding import PartitionSpec as P

CHUNKS = 4
VMEM_LIMIT = 16 << 20
VMEM = pl.BlockSpec(memory_space=pltpu.VMEM)
HBM = pl.BlockSpec(memory_space=pltpu.HBM)
PARAMS = pltpu.CompilerParams(vmem_limit_bytes=VMEM_LIMIT)


def nu_order(size):
    return [(12 + p) % size for p in range(size)]


def lam_order(size):
    return [(45 + p) % size for p in range(size)]


def first_kernel(integrals_hbm, orbitals_hbm, out_ref, orbitals, integrals, sems):
    lams, mus, ns = integrals.shape
    owners = out_ref.shape[0]
    size = mus // CHUNKS
    copies = []
    for c in range(CHUNKS):
        rows = pl.ds(c * size, size)
        copies.append(
            (
                pltpu.make_async_copy(orbitals_hbm.at[rows], orbitals.at[rows], sems.at[0, c]),
                pltpu.make_async_copy(integrals_hbm.at[:, rows], integrals.at[:, rows], sems.at[1, c]),
            )
        )
    for pair in copies:
        for copy in pair:
            copy.start()
    total = None
    for c in range(CHUNKS):
        for copy in copies[c]:
            copy.wait()
        rows = pl.ds(c * size, size)
        block = jnp.concatenate([integrals[l, rows, :].T for l in range(lams)], axis=0)
        term = jnp.dot(block, orbitals[rows, :], preferred_element_type=jnp.float32)
        total = term if total is None else total + term
    total = total.astype(out_ref.dtype)
    width = total.shape[1] // owners
    for l in range(lams):
        block = total[l * ns : (l + 1) * ns].T
        for p, owner in enumerate(nu_order(owners)):
            out_ref[p, l * width : (l + 1) * width, :] = block[owner * width : (owner + 1) * width]


def first(integrals, orbitals, owners):
    lams, _, ns = integrals.shape
    orbs = orbitals.shape[1]
    return pl.pallas_call(
        first_kernel,
        out_shape=(
            pltpu.VMEM((owners, lams * orbs // owners, ns), integrals.dtype),
            pltpu.VMEM(orbitals.shape, orbitals.dtype),
        ),
        in_specs=[HBM, HBM],
        out_specs=(VMEM, VMEM),
        scratch_shapes=[
            pltpu.VMEM(integrals.shape, integrals.dtype),
            pltpu.SemaphoreType.DMA((2, CHUNKS)),
        ],
        compiler_params=PARAMS,
    )(*(pltpu.with_memory_space_constraint(x, pltpu.HBM) for x in (integrals, orbitals)))


def second_kernel(weights_ref, rows_ref, orbitals_ref, out_ref):
    lams, korb = weights_ref.shape
    owners, height, ns = rows_ref.shape
    place = {owner: p for p, owner in enumerate(nu_order(owners))}
    step = 2
    total = None
    for s in range(0, owners, step):
        left = jnp.concatenate([rows_ref[place[s + t]] for t in range(step)], axis=1)
        right = orbitals_ref[s * ns : (s + step) * ns, :]
        term = jnp.dot(left, right, preferred_element_type=jnp.float32)
        total = term if total is None else total + term
    width = height // lams
    weights = weights_ref[...].astype(jnp.float32)
    terms = []
    for k in range(korb):
        term = weights[0:1, k : k + 1] * total[:width]
        for l in range(1, lams):
            term = term + weights[l : l + 1, k : k + 1] * total[l * width : (l + 1) * width]
        terms.append(term)
    sent = jnp.concatenate(terms, axis=0).astype(out_ref.dtype).T
    sent = sent.reshape(out_ref.shape)
    for p, owner in enumerate(lam_order(out_ref.shape[0])):
        out_ref[p] = sent[owner]


def second(weights, rows, orbitals, owners):
    _, height, _ = rows.shape
    lams, korb = weights.shape
    orbs = orbitals.shape[1]
    return pl.pallas_call(
        second_kernel,
        out_shape=pltpu.VMEM((owners, orbs // owners, korb * height // lams), rows.dtype),
        in_specs=[VMEM, VMEM, VMEM],
        out_specs=VMEM,
        compiler_params=PARAMS,
    )(*(pltpu.with_memory_space_constraint(x, pltpu.VMEM) for x in (weights, rows, orbitals)))


def last_kernel(terms_ref, out_ref):
    korb, _, width = out_ref.shape
    total = jnp.sum(terms_ref[...].astype(jnp.float32), axis=0)
    for k in range(korb):
        out_ref[k] = total[:, k * width : (k + 1) * width]


def last(terms, korb):
    _, js, height = terms.shape
    return pl.pallas_call(
        last_kernel,
        out_shape=jax.ShapeDtypeStruct((korb, js, height // korb), jnp.float32),
        in_specs=[VMEM],
        out_specs=VMEM,
        compiler_params=PARAMS,
    )(pltpu.with_memory_space_constraint(terms, pltpu.VMEM))


def exchange(blocks, axis, order):
    return lax.all_to_all(blocks, axis, split_axis=0, concat_axis=0, tiled=True, axis_index_groups=[order])


def shards(lam_owners, nu_owners, integrals, orbitals, lam_orbitals):
    halfway, orbitals = first(integrals, orbitals, nu_owners)
    rows = exchange(halfway, "nu", nu_order(nu_owners))
    sent = second(lam_orbitals, rows, orbitals, lam_owners)
    terms = exchange(sent, "lam", lam_order(lam_owners))
    return last(terms, lam_orbitals.shape[1]).transpose(0, 2, 1)


def solution(mesh):
    return jax.shard_map(
        functools.partial(shards, mesh.shape["lam"], mesh.shape["nu"]),
        mesh=mesh,
        in_specs=(P("lam", None, "nu"), P(), P("lam", None)),
        out_specs=P(None, "nu", "lam"),
        check_vma=False,
    )
```

```python
import functools

import jax
import jax.numpy as jnp
from jax import lax
from jax.experimental import pallas as pl
from jax.experimental.pallas import tpu as pltpu
from jax.sharding import PartitionSpec as P

CHUNKS = 4
VMEM_LIMIT = 16 << 20
VMEM = pl.BlockSpec(memory_space=pltpu.VMEM)
HBM = pl.BlockSpec(memory_space=pltpu.HBM)
PARAMS = pltpu.CompilerParams(vmem_limit_bytes=VMEM_LIMIT)


def nu_order(size):
    return [(12 + p) % size for p in range(size)]


def lam_order(size):
    return [(45 + p) % size for p in range(size)]


def first_kernel(integrals_hbm, orbitals_hbm, out_ref, orbitals, integrals, sems):
    lams, mus, ns = integrals.shape
    owners = out_ref.shape[0]
    size = mus // CHUNKS
    copies = []
    for c in range(CHUNKS):
        rows = pl.ds(c * size, size)
        copies.append(
            (
                pltpu.make_async_copy(orbitals_hbm.at[rows], orbitals.at[rows], sems.at[0, c]),
                pltpu.make_async_copy(integrals_hbm.at[:, rows], integrals.at[:, rows], sems.at[1, c]),
            )
        )
    for pair in copies:
        for copy in pair:
            copy.start()
    total = None
    for c in range(CHUNKS):
        for copy in copies[c]:
            copy.wait()
        rows = pl.ds(c * size, size)
        block = jnp.concatenate([integrals[l, rows, :].T for l in range(lams)], axis=0)
        term = jnp.dot(block, orbitals[rows, :], preferred_element_type=jnp.float32)
        total = term if total is None else total + term
    total = total.astype(out_ref.dtype)
    width = total.shape[1] // owners
    for l in range(lams):
        block = total[l * ns : (l + 1) * ns].T
        for p, owner in enumerate(nu_order(owners)):
            out_ref[p, l * width : (l + 1) * width, :] = block[owner * width : (owner + 1) * width]


def first(integrals, orbitals, owners):
    lams, _, ns = integrals.shape
    orbs = orbitals.shape[1]
    return pl.pallas_call(
        first_kernel,
        out_shape=(
            pltpu.VMEM((owners, lams * orbs // owners, ns), integrals.dtype),
            pltpu.VMEM(orbitals.shape, orbitals.dtype),
        ),
        in_specs=[HBM, HBM],
        out_specs=(VMEM, VMEM),
        scratch_shapes=[
            pltpu.VMEM(integrals.shape, integrals.dtype),
            pltpu.SemaphoreType.DMA((2, CHUNKS)),
        ],
        compiler_params=PARAMS,
    )(*(pltpu.with_memory_space_constraint(x, pltpu.HBM) for x in (integrals, orbitals)))


def second_kernel(weights_ref, rows_ref, orbitals_ref, out_ref):
    lams, korb = weights_ref.shape
    owners, height, ns = rows_ref.shape
    place = {owner: p for p, owner in enumerate(nu_order(owners))}
    step = 2
    total = None
    for s in range(0, owners, step):
        left = jnp.concatenate([rows_ref[place[s + t]] for t in range(step)], axis=1)
        right = orbitals_ref[s * ns : (s + step) * ns, :]
        term = jnp.dot(left, right, preferred_element_type=jnp.float32)
        total = term if total is None else total + term
    half = orbitals_ref.shape[1] // out_ref.shape[0] // 2
    sent = total.T.reshape(out_ref.shape[0], 2 * half, height)
    sent = jnp.concatenate([sent[:, :half], sent[:, half:]], axis=2).astype(out_ref.dtype)
    weights = weights_ref[...].astype(jnp.float32)
    width = height // lams
    lanes = [
        jnp.concatenate([jnp.broadcast_to(weights[l : l + 1, k : k + 1], (1, width)) for l in range(lams)], axis=1)
        for k in range(korb)
    ]
    spread = jnp.concatenate(
        [jnp.concatenate(lanes[k : k + 2], axis=1) for k in range(0, korb, 2)], axis=0
    ).astype(out_ref.dtype)
    for p, owner in enumerate(lam_order(out_ref.shape[0])):
        for g in range(half // 2):
            out_ref[p, g] = sent[owner, 2 * g : 2 * g + 2]
        out_ref[p, half // 2] = spread


def second(weights, rows, orbitals, owners):
    _, height, _ = rows.shape
    lams, korb = weights.shape
    orbs = orbitals.shape[1]
    return pl.pallas_call(
        second_kernel,
        out_shape=pltpu.VMEM((owners, orbs // owners // 4 + 1, 2, 2 * height), rows.dtype),
        in_specs=[VMEM, VMEM, VMEM],
        out_specs=VMEM,
        compiler_params=PARAMS,
    )(*(pltpu.with_memory_space_constraint(x, pltpu.VMEM) for x in (weights, rows, orbitals)))


def last_kernel(terms_ref, out_ref):
    korb, js, width = out_ref.shape
    owners, groups, pair, wide = terms_ref.shape
    lanes = wide // 2
    rows = [terms_ref[:, g].reshape(owners * pair, wide).astype(jnp.float32) for g in range(groups)]
    own = rows.pop()
    even = lax.rem(lax.broadcasted_iota(jnp.int32, own.shape, 0), pair) == 0
    low = lax.broadcasted_iota(jnp.int32, own.shape, 1) < lanes
    count = owners * pair
    for r in range(pair):
        near = jnp.where(even, own, pltpu.roll(own, 1, 0)) if r == 0 else jnp.where(even, pltpu.roll(own, count - 1, 0), own)
        far = pltpu.roll(near, lanes, 1)
        for side in range(2):
            k = 2 * r + side
            weight = jnp.where(low, near, far) if side == 0 else jnp.where(low, far, near)
            for g in range(groups - 1):
                total = jnp.sum((rows[g] * weight).reshape(count // 8, 8, wide), axis=0)
                total = total[0:2] + total[2:4] + total[4:6] + total[6:8]
                for h in range(2):
                    block = total[:, h * lanes : (h + 1) * lanes]
                    value = block[:, :width]
                    for l in range(1, lanes // width):
                        value = value + block[:, l * width : (l + 1) * width]
                    row = h * (js // 2) + 2 * g
                    out_ref[k, row : row + 2] = value


def last(terms, korb, js, width):
    return pl.pallas_call(
        last_kernel,
        out_shape=jax.ShapeDtypeStruct((korb, js, width), jnp.float32),
        in_specs=[VMEM],
        out_specs=VMEM,
        compiler_params=PARAMS,
    )(pltpu.with_memory_space_constraint(terms, pltpu.VMEM))


def exchange(blocks, axis, order):
    return lax.all_to_all(blocks, axis, split_axis=0, concat_axis=0, tiled=True, axis_index_groups=[order])


def shards(lam_owners, nu_owners, integrals, orbitals, lam_orbitals):
    halfway, orbitals = first(integrals, orbitals, nu_owners)
    rows = exchange(halfway, "nu", nu_order(nu_owners))
    sent = second(lam_orbitals, rows, orbitals, lam_owners)
    terms = exchange(sent, "lam", lam_order(lam_owners))
    orbs = orbitals.shape[1]
    return last(terms, lam_orbitals.shape[1], orbs // lam_owners, orbs // nu_owners).transpose(0, 2, 1)


def solution(mesh):
    return jax.shard_map(
        functools.partial(shards, mesh.shape["lam"], mesh.shape["nu"]),
        mesh=mesh,
        in_specs=(P("lam", None, "nu"), P(), P("lam", None)),
        out_specs=P(None, "nu", "lam"),
        check_vma=False,
    )
```

```python
import functools

import jax
import jax.numpy as jnp
from jax import lax
from jax.experimental import pallas as pl
from jax.experimental.pallas import tpu as pltpu
from jax.sharding import PartitionSpec as P

CHUNKS = 4
VMEM_LIMIT = 16 << 20
VMEM = pl.BlockSpec(memory_space=pltpu.VMEM)
HBM = pl.BlockSpec(memory_space=pltpu.HBM)
PARAMS = pltpu.CompilerParams(vmem_limit_bytes=VMEM_LIMIT)


def nu_order(size):
    return [(12 + p) % size for p in range(size)]


def lam_order(size):
    return [(45 + p) % size for p in range(size)]


def first_kernel(integrals_hbm, orbitals_hbm, out_ref, orbitals, integrals, sems):
    lams, mus, ns = integrals.shape
    owners = out_ref.shape[0]
    size = mus // CHUNKS
    copies = []
    for c in range(CHUNKS):
        rows = pl.ds(c * size, size)
        copies.append(
            (
                pltpu.make_async_copy(orbitals_hbm.at[rows], orbitals.at[rows], sems.at[0, c]),
                pltpu.make_async_copy(integrals_hbm.at[:, rows], integrals.at[:, rows], sems.at[1, c]),
            )
        )
    for pair in copies:
        for copy in pair:
            copy.start()
    total = None
    for c in range(CHUNKS):
        for copy in copies[c]:
            copy.wait()
        rows = pl.ds(c * size, size)
        block = jnp.concatenate([integrals[l, rows, :].T for l in range(lams)], axis=0)
        term = jnp.dot(block, orbitals[rows, :], preferred_element_type=jnp.float32)
        total = term if total is None else total + term
    total = total.astype(out_ref.dtype)
    width = total.shape[1] // owners
    for l in range(lams):
        block = total[l * ns : (l + 1) * ns].T
        for p, owner in enumerate(nu_order(owners)):
            out_ref[p, l * width : (l + 1) * width, :] = block[owner * width : (owner + 1) * width]


def first(integrals, orbitals, owners):
    lams, _, ns = integrals.shape
    orbs = orbitals.shape[1]
    return pl.pallas_call(
        first_kernel,
        out_shape=(
            pltpu.VMEM((owners, lams * orbs // owners, ns), integrals.dtype),
            pltpu.VMEM(orbitals.shape, orbitals.dtype),
        ),
        in_specs=[HBM, HBM],
        out_specs=(VMEM, VMEM),
        scratch_shapes=[
            pltpu.VMEM(integrals.shape, integrals.dtype),
            pltpu.SemaphoreType.DMA((2, CHUNKS)),
        ],
        compiler_params=PARAMS,
    )(*(pltpu.with_memory_space_constraint(x, pltpu.HBM) for x in (integrals, orbitals)))


def second_kernel(weights_ref, rows_ref, orbitals_ref, out_ref):
    lams, korb = weights_ref.shape
    owners, height, ns = rows_ref.shape
    place = {owner: p for p, owner in enumerate(nu_order(owners))}
    left = jnp.concatenate([rows_ref[place[owner]] for owner in range(owners)], axis=1)
    total = jnp.dot(left, orbitals_ref[...], preferred_element_type=jnp.float32)
    half = orbitals_ref.shape[1] // out_ref.shape[0] // 2
    sent = total.T.reshape(out_ref.shape[0], 2 * half, height)
    sent = jnp.concatenate([sent[:, :half], sent[:, half:]], axis=2).astype(out_ref.dtype)
    weights = weights_ref[...].astype(jnp.float32)
    width = height // lams
    lanes = [
        jnp.concatenate([jnp.broadcast_to(weights[l : l + 1, k : k + 1], (1, width)) for l in range(lams)], axis=1)
        for k in range(korb)
    ]
    spread = jnp.concatenate(
        [jnp.concatenate(lanes[k : k + 2], axis=1) for k in range(0, korb, 2)], axis=0
    ).astype(out_ref.dtype)
    for p, owner in enumerate(lam_order(out_ref.shape[0])):
        for g in range(half // 2):
            out_ref[p, g] = sent[owner, 2 * g : 2 * g + 2]
        out_ref[p, half // 2] = spread


def second(weights, rows, orbitals, owners):
    _, height, _ = rows.shape
    lams, korb = weights.shape
    orbs = orbitals.shape[1]
    return pl.pallas_call(
        second_kernel,
        out_shape=pltpu.VMEM((owners, orbs // owners // 4 + 1, 2, 2 * height), rows.dtype),
        in_specs=[VMEM, VMEM, VMEM],
        out_specs=VMEM,
        compiler_params=PARAMS,
    )(*(pltpu.with_memory_space_constraint(x, pltpu.VMEM) for x in (weights, rows, orbitals)))


def last_kernel(terms_ref, out_ref):
    korb, js, width = out_ref.shape
    owners, groups, pair, wide = terms_ref.shape
    lanes = wide // 2
    rows = [terms_ref[:, g].reshape(owners * pair, wide).astype(jnp.float32) for g in range(groups)]
    own = rows.pop()
    even = lax.rem(lax.broadcasted_iota(jnp.int32, own.shape, 0), pair) == 0
    low = lax.broadcasted_iota(jnp.int32, own.shape, 1) < lanes
    count = owners * pair
    for r in range(pair):
        near = jnp.where(even, own, pltpu.roll(own, 1, 0)) if r == 0 else jnp.where(even, pltpu.roll(own, count - 1, 0), own)
        far = pltpu.roll(near, lanes, 1)
        for side in range(2):
            k = 2 * r + side
            weight = jnp.where(low, near, far) if side == 0 else jnp.where(low, far, near)
            for g in range(groups - 1):
                total = jnp.sum((rows[g] * weight).reshape(count // 8, 8, wide), axis=0)
                total = total[0:2] + total[2:4] + total[4:6] + total[6:8]
                for h in range(2):
                    block = total[:, h * lanes : (h + 1) * lanes]
                    value = block[:, :width]
                    for l in range(1, lanes // width):
                        value = value + block[:, l * width : (l + 1) * width]
                    row = h * (js // 2) + 2 * g
                    out_ref[k, row : row + 2] = value


def last(terms, korb, js, width):
    return pl.pallas_call(
        last_kernel,
        out_shape=jax.ShapeDtypeStruct((korb, js, width), jnp.float32),
        in_specs=[VMEM],
        out_specs=VMEM,
        compiler_params=PARAMS,
    )(pltpu.with_memory_space_constraint(terms, pltpu.VMEM))


def exchange(blocks, axis, order):
    return lax.all_to_all(blocks, axis, split_axis=0, concat_axis=0, tiled=True, axis_index_groups=[order])


def shards(lam_owners, nu_owners, integrals, orbitals, lam_orbitals):
    halfway, orbitals = first(integrals, orbitals, nu_owners)
    rows = exchange(halfway, "nu", nu_order(nu_owners))
    sent = second(lam_orbitals, rows, orbitals, lam_owners)
    terms = exchange(sent, "lam", lam_order(lam_owners))
    orbs = orbitals.shape[1]
    return last(terms, lam_orbitals.shape[1], orbs // lam_owners, orbs // nu_owners).transpose(0, 2, 1)


def solution(mesh):
    return jax.shard_map(
        functools.partial(shards, mesh.shape["lam"], mesh.shape["nu"]),
        mesh=mesh,
        in_specs=(P("lam", None, "nu"), P(), P("lam", None)),
        out_specs=P(None, "nu", "lam"),
        check_vma=False,
    )
```

```python
import functools

import jax
import jax.numpy as jnp
from jax import lax
from jax.experimental import pallas as pl
from jax.experimental.pallas import tpu as pltpu
from jax.sharding import PartitionSpec as P

CHUNKS = 4
VMEM_LIMIT = 16 << 20
VMEM = pl.BlockSpec(memory_space=pltpu.VMEM)
HBM = pl.BlockSpec(memory_space=pltpu.HBM)
PARAMS = pltpu.CompilerParams(vmem_limit_bytes=VMEM_LIMIT)


def nu_order(size):
    return [(12 + p) % size for p in range(size)]


def lam_order(size):
    return [(61 + p) % size for p in range(size)]


def first_kernel(integrals_hbm, orbitals_hbm, out_ref, orbitals, integrals, sems):
    lams, mus, ns = integrals.shape
    owners = out_ref.shape[0]
    size = mus // CHUNKS
    copies = []
    for c in range(CHUNKS):
        rows = pl.ds(c * size, size)
        copies.append(
            (
                pltpu.make_async_copy(orbitals_hbm.at[rows], orbitals.at[rows], sems.at[0, c]),
                pltpu.make_async_copy(integrals_hbm.at[:, rows], integrals.at[:, rows], sems.at[1, c]),
            )
        )
    for pair in copies:
        for copy in pair:
            copy.start()
    total = None
    for c in range(CHUNKS):
        for copy in copies[c]:
            copy.wait()
        rows = pl.ds(c * size, size)
        block = jnp.concatenate([integrals[l, rows, :].T for l in range(lams)], axis=0)
        term = jnp.dot(block, orbitals[rows, :], preferred_element_type=jnp.float32)
        total = term if total is None else total + term
    total = total.astype(out_ref.dtype)
    width = total.shape[1] // owners
    for l in range(lams):
        block = total[l * ns : (l + 1) * ns].T
        for p, owner in enumerate(nu_order(owners)):
            out_ref[p, l * width : (l + 1) * width, :] = block[owner * width : (owner + 1) * width]


def first(integrals, orbitals, owners):
    lams, _, ns = integrals.shape
    orbs = orbitals.shape[1]
    return pl.pallas_call(
        first_kernel,
        out_shape=(
            pltpu.VMEM((owners, lams * orbs // owners, ns), integrals.dtype),
            pltpu.VMEM(orbitals.shape, orbitals.dtype),
        ),
        in_specs=[HBM, HBM],
        out_specs=(VMEM, VMEM),
        scratch_shapes=[
            pltpu.VMEM(integrals.shape, integrals.dtype),
            pltpu.SemaphoreType.DMA((2, CHUNKS)),
        ],
        compiler_params=PARAMS,
    )(*(pltpu.with_memory_space_constraint(x, pltpu.HBM) for x in (integrals, orbitals)))


def second_kernel(weights_ref, rows_ref, orbitals_ref, out_ref):
    lams, korb = weights_ref.shape
    owners, height, ns = rows_ref.shape
    place = {owner: p for p, owner in enumerate(nu_order(owners))}
    left = jnp.concatenate([rows_ref[place[owner]] for owner in range(owners)], axis=1)
    total = jnp.dot(left, orbitals_ref[...], preferred_element_type=jnp.float32)
    half = orbitals_ref.shape[1] // out_ref.shape[0] // 2
    sent = total.T.reshape(out_ref.shape[0], 2 * half, height)
    sent = jnp.concatenate([sent[:, :half], sent[:, half:]], axis=2).astype(out_ref.dtype)
    weights = weights_ref[...].astype(jnp.float32)
    width = height // lams
    lanes = [
        jnp.concatenate([jnp.broadcast_to(weights[l : l + 1, k : k + 1], (1, width)) for l in range(lams)], axis=1)
        for k in range(korb)
    ]
    spread = jnp.concatenate(
        [jnp.concatenate(lanes[k : k + 2], axis=1) for k in range(0, korb, 2)], axis=0
    ).astype(out_ref.dtype)
    for p, owner in enumerate(lam_order(out_ref.shape[0])):
        for g in range(half // 2):
            out_ref[p, g] = sent[owner, 2 * g : 2 * g + 2]
        out_ref[p, half // 2] = spread


def second(weights, rows, orbitals, owners):
    _, height, _ = rows.shape
    lams, korb = weights.shape
    orbs = orbitals.shape[1]
    return pl.pallas_call(
        second_kernel,
        out_shape=pltpu.VMEM((owners, orbs // owners // 4 + 1, 2, 2 * height), rows.dtype),
        in_specs=[VMEM, VMEM, VMEM],
        out_specs=VMEM,
        compiler_params=PARAMS,
    )(*(pltpu.with_memory_space_constraint(x, pltpu.VMEM) for x in (weights, rows, orbitals)))


def last_kernel(terms_ref, out_ref):
    korb, js, width = out_ref.shape
    owners, groups, pair, wide = terms_ref.shape
    lanes = wide // 2
    rows = [terms_ref[:, g].reshape(owners * pair, wide).astype(jnp.float32) for g in range(groups)]
    own = rows.pop()
    even = lax.rem(lax.broadcasted_iota(jnp.int32, own.shape, 0), pair) == 0
    low = lax.broadcasted_iota(jnp.int32, own.shape, 1) < lanes
    count = owners * pair
    for r in range(pair):
        near = jnp.where(even, own, pltpu.roll(own, 1, 0)) if r == 0 else jnp.where(even, pltpu.roll(own, count - 1, 0), own)
        far = pltpu.roll(near, lanes, 1)
        for side in range(2):
            k = 2 * r + side
            weight = jnp.where(low, near, far) if side == 0 else jnp.where(low, far, near)
            for g in range(groups - 1):
                total = jnp.sum((rows[g] * weight).reshape(count // 8, 8, wide), axis=0)
                total = total[0:2] + total[2:4] + total[4:6] + total[6:8]
                for h in range(2):
                    block = total[:, h * lanes : (h + 1) * lanes]
                    value = block[:, :width]
                    for l in range(1, lanes // width):
                        value = value + block[:, l * width : (l + 1) * width]
                    row = h * (js // 2) + 2 * g
                    out_ref[k, row : row + 2] = value


def last(terms, korb, js, width):
    return pl.pallas_call(
        last_kernel,
        out_shape=jax.ShapeDtypeStruct((korb, js, width), jnp.float32),
        in_specs=[VMEM],
        out_specs=VMEM,
        compiler_params=PARAMS,
    )(pltpu.with_memory_space_constraint(terms, pltpu.VMEM))


def exchange(blocks, axis, order):
    return lax.all_to_all(blocks, axis, split_axis=0, concat_axis=0, tiled=True, axis_index_groups=[order])


def shards(lam_owners, nu_owners, integrals, orbitals, lam_orbitals):
    halfway, orbitals = first(integrals, orbitals, nu_owners)
    rows = exchange(halfway, "nu", nu_order(nu_owners))
    sent = second(lam_orbitals, rows, orbitals, lam_owners)
    terms = exchange(sent, "lam", lam_order(lam_owners))
    orbs = orbitals.shape[1]
    return last(terms, lam_orbitals.shape[1], orbs // lam_owners, orbs // nu_owners).transpose(0, 2, 1)


def solution(mesh):
    return jax.shard_map(
        functools.partial(shards, mesh.shape["lam"], mesh.shape["nu"]),
        mesh=mesh,
        in_specs=(P("lam", None, "nu"), P(), P("lam", None)),
        out_specs=P(None, "nu", "lam"),
        check_vma=False,
    )
```

```python
import functools

import jax
import jax.numpy as jnp
from jax import lax
from jax.experimental import pallas as pl
from jax.experimental.pallas import tpu as pltpu
from jax.sharding import PartitionSpec as P

CHUNKS = 4
VMEM_LIMIT = 16 << 20
VMEM = pl.BlockSpec(memory_space=pltpu.VMEM)
HBM = pl.BlockSpec(memory_space=pltpu.HBM)
PARAMS = pltpu.CompilerParams(vmem_limit_bytes=VMEM_LIMIT)


def nu_order(size):
    return [(12 - p) % size for p in range(size)]


def lam_order(size):
    return [(45 + p) % size for p in range(size)]


def first_kernel(integrals_hbm, orbitals_hbm, out_ref, orbitals, integrals, sems):
    lams, mus, ns = integrals.shape
    owners = out_ref.shape[0]
    size = mus // CHUNKS
    copies = []
    for c in range(CHUNKS):
        rows = pl.ds(c * size, size)
        copies.append(
            (
                pltpu.make_async_copy(orbitals_hbm.at[rows], orbitals.at[rows], sems.at[0, c]),
                pltpu.make_async_copy(integrals_hbm.at[:, rows], integrals.at[:, rows], sems.at[1, c]),
            )
        )
    for pair in copies:
        for copy in pair:
            copy.start()
    total = None
    for c in range(CHUNKS):
        for copy in copies[c]:
            copy.wait()
        rows = pl.ds(c * size, size)
        block = jnp.concatenate([integrals[l, rows, :].T for l in range(lams)], axis=0)
        term = jnp.dot(block, orbitals[rows, :], preferred_element_type=jnp.float32)
        total = term if total is None else total + term
    total = total.astype(out_ref.dtype)
    width = total.shape[1] // owners
    for l in range(lams):
        block = total[l * ns : (l + 1) * ns].T
        for p, owner in enumerate(nu_order(owners)):
            out_ref[p, l * width : (l + 1) * width, :] = block[owner * width : (owner + 1) * width]


def first(integrals, orbitals, owners):
    lams, _, ns = integrals.shape
    orbs = orbitals.shape[1]
    return pl.pallas_call(
        first_kernel,
        out_shape=(
            pltpu.VMEM((owners, lams * orbs // owners, ns), integrals.dtype),
            pltpu.VMEM(orbitals.shape, orbitals.dtype),
        ),
        in_specs=[HBM, HBM],
        out_specs=(VMEM, VMEM),
        scratch_shapes=[
            pltpu.VMEM(integrals.shape, integrals.dtype),
            pltpu.SemaphoreType.DMA((2, CHUNKS)),
        ],
        compiler_params=PARAMS,
    )(*(pltpu.with_memory_space_constraint(x, pltpu.HBM) for x in (integrals, orbitals)))


def second_kernel(weights_ref, rows_ref, orbitals_ref, out_ref):
    lams, korb = weights_ref.shape
    owners, height, ns = rows_ref.shape
    place = {owner: p for p, owner in enumerate(nu_order(owners))}
    left = jnp.concatenate([rows_ref[place[owner]] for owner in range(owners)], axis=1)
    total = jnp.dot(left, orbitals_ref[...], preferred_element_type=jnp.float32)
    half = orbitals_ref.shape[1] // out_ref.shape[0] // 2
    sent = total.T.reshape(out_ref.shape[0], 2 * half, height)
    sent = jnp.concatenate([sent[:, :half], sent[:, half:]], axis=2).astype(out_ref.dtype)
    weights = weights_ref[...].astype(jnp.float32)
    width = height // lams
    lanes = [
        jnp.concatenate([jnp.broadcast_to(weights[l : l + 1, k : k + 1], (1, width)) for l in range(lams)], axis=1)
        for k in range(korb)
    ]
    spread = jnp.concatenate(
        [jnp.concatenate(lanes[k : k + 2], axis=1) for k in range(0, korb, 2)], axis=0
    ).astype(out_ref.dtype)
    for p, owner in enumerate(lam_order(out_ref.shape[0])):
        for g in range(half // 2):
            out_ref[p, g] = sent[owner, 2 * g : 2 * g + 2]
        out_ref[p, half // 2] = spread


def second(weights, rows, orbitals, owners):
    _, height, _ = rows.shape
    lams, korb = weights.shape
    orbs = orbitals.shape[1]
    return pl.pallas_call(
        second_kernel,
        out_shape=pltpu.VMEM((owners, orbs // owners // 4 + 1, 2, 2 * height), rows.dtype),
        in_specs=[VMEM, VMEM, VMEM],
        out_specs=VMEM,
        compiler_params=PARAMS,
    )(*(pltpu.with_memory_space_constraint(x, pltpu.VMEM) for x in (weights, rows, orbitals)))


def last_kernel(terms_ref, out_ref):
    korb, js, width = out_ref.shape
    owners, groups, pair, wide = terms_ref.shape
    lanes = wide // 2
    rows = [terms_ref[:, g].reshape(owners * pair, wide).astype(jnp.float32) for g in range(groups)]
    own = rows.pop()
    even = lax.rem(lax.broadcasted_iota(jnp.int32, own.shape, 0), pair) == 0
    low = lax.broadcasted_iota(jnp.int32, own.shape, 1) < lanes
    count = owners * pair
    for r in range(pair):
        near = jnp.where(even, own, pltpu.roll(own, 1, 0)) if r == 0 else jnp.where(even, pltpu.roll(own, count - 1, 0), own)
        far = pltpu.roll(near, lanes, 1)
        for side in range(2):
            k = 2 * r + side
            weight = jnp.where(low, near, far) if side == 0 else jnp.where(low, far, near)
            for g in range(groups - 1):
                total = jnp.sum((rows[g] * weight).reshape(count // 8, 8, wide), axis=0)
                total = total[0:2] + total[2:4] + total[4:6] + total[6:8]
                for h in range(2):
                    block = total[:, h * lanes : (h + 1) * lanes]
                    value = block[:, :width]
                    for l in range(1, lanes // width):
                        value = value + block[:, l * width : (l + 1) * width]
                    row = h * (js // 2) + 2 * g
                    out_ref[k, row : row + 2] = value


def last(terms, korb, js, width):
    return pl.pallas_call(
        last_kernel,
        out_shape=jax.ShapeDtypeStruct((korb, js, width), jnp.float32),
        in_specs=[VMEM],
        out_specs=VMEM,
        compiler_params=PARAMS,
    )(pltpu.with_memory_space_constraint(terms, pltpu.VMEM))


def exchange(blocks, axis, order):
    return lax.all_to_all(blocks, axis, split_axis=0, concat_axis=0, tiled=True, axis_index_groups=[order])


def shards(lam_owners, nu_owners, integrals, orbitals, lam_orbitals):
    halfway, orbitals = first(integrals, orbitals, nu_owners)
    rows = exchange(halfway, "nu", nu_order(nu_owners))
    sent = second(lam_orbitals, rows, orbitals, lam_owners)
    terms = exchange(sent, "lam", lam_order(lam_owners))
    orbs = orbitals.shape[1]
    return last(terms, lam_orbitals.shape[1], orbs // lam_owners, orbs // nu_owners).transpose(0, 2, 1)


def solution(mesh):
    return jax.shard_map(
        functools.partial(shards, mesh.shape["lam"], mesh.shape["nu"]),
        mesh=mesh,
        in_specs=(P("lam", None, "nu"), P(), P("lam", None)),
        out_specs=P(None, "nu", "lam"),
        check_vma=False,
    )
```
